32 devices in a mesh: grp: 4 (over x, core), blk: 8 (over z, y).
Axes of the slice: x: 2, y: 2, z: 4, core: 2. Of those that a mesh axis runs over, the one named last changes fastest.
Arguments:
- targets: float32 [16, 262144], P('blk', 'grp'), may hold values from -6 to 6
- sources: float32 [32, 262144], P(('grp', 'blk')), may hold values from -6 to 6
- occupation: int32 [32], P(('grp', 'blk')), may hold values from 1 to 2
- offsets: int32 [4], replicated, may hold values from 0 to 7, as said below
Outputs:
- exchange: float32 [16, 262144], P('blk', 'grp')
The draws below stay inside these ranges and needn't reach their ends.
Inputs may be any that keep to these rules, and one draw needn't show every extreme that they name: The groups' offsets are distinct and the largest is 7.
All inputs are finite; a program needn't handle non-finite values.
Results may differ from the reference program's by a relative error of at most 0.0003.
Values sent between devices are 32-bit elements; how exact they have to be, the bound alone decides.
A program may use at most 128 MiB of HBM per device.

```python
import math
import jax
import jax.numpy as jnp
from jax import lax

NG = 64
CELLS = 262144
TGT_DEV = 2
SRC_DEV = 1
STOPS = 4
GROUPS = 4
CYCLE = 8
TGT = 16
NSRC = 32


def draw_offsets(key, part):
    ordering = jax.random.permutation(key, jnp.arange(CYCLE, dtype=jnp.int32))[:GROUPS]
    return (ordering + (CYCLE - 1 - jnp.max(ordering))).astype(jnp.int32)


def plant(drawn, key, least, top_value):
    shape = drawn.shape
    place = [jax.random.randint(jax.random.fold_in(key, axis), (), 0, shape[axis]) for axis in range(len(shape))]
    drawn = drawn.at[tuple(place)].set(least)
    longest = shape.index(max(shape))
    place[longest] = (place[longest] + 1) % shape[longest]
    return drawn.at[tuple(place)].set(top_value)


def block_levels(own_key, shape, pieces, low, top_value):
    level, own = 1.0, jax.random.fold_in(own_key, 6)
    for axis_at, blocks in pieces:
        heights = jnp.exp(jax.random.uniform(jax.random.fold_in(own, axis_at), (blocks,), jnp.float32, low / len(pieces), top_value / len(pieces)))
        level = level * jnp.repeat(heights, shape[axis_at] // blocks).reshape([-1 if axis == axis_at else 1 for axis in range(len(shape))])
    return level


def centred(rng, dims, spread, bound, split=(), kind=jnp.bfloat16):
    array = spread * jax.random.normal(rng, dims, jnp.float32)
    if split:
        array = array * block_levels(rng, dims, split, -0.22, 0.18)
    return jnp.clip(array, -bound, bound).astype(kind)


def setup_inputs(seed: int = 0) -> dict:
    seeds = jax.random.split(jax.random.key(seed), 5)
    return {
        "targets": centred(seeds[0], (TGT, CELLS), 1.0, 6.0, ((0, 8), (1, 4)), jnp.float32),
        "sources": centred(seeds[1], (NSRC, CELLS), 1.0, 6.0, ((0, 32),), jnp.float32),
        "occupation": plant(jax.random.randint(seeds[2], (NSRC,), 1, 3), jax.random.fold_in(seeds[2], 1), 1, 2).astype(jnp.int32),
        "offsets": draw_offsets(jax.random.fold_in(seeds[4], 71), 0),
    }


box_length = 16.0
screen_square = 0.25

def screened_kernel(grid_size):
    counter = jnp.arange(grid_size, dtype=jnp.int32)
    signed_freq = jnp.where(counter < grid_size // 2, counter, counter - grid_size).astype(jnp.float32)
    wave_number = 2.0 * math.pi * signed_freq / box_length
    wave_square = wave_number * wave_number
    summed = wave_square[:, None, None] + wave_square[None, :, None] + wave_square[None, None, :]
    return 4.0 * math.pi / (summed + screen_square)

def pair_potential(density, kernel_grid):
    lead_shape = density.shape[:-1]
    cube_field = density.reshape(lead_shape + (NG, NG, NG))
    spectrum = jnp.fft.fftn(cube_field, axes=(-3, -2, -1))
    potential = jnp.real(jnp.fft.ifftn(spectrum * kernel_grid, axes=(-3, -2, -1)))
    return potential.astype(jnp.float32).reshape(lead_shape + (CELLS,))

def reference(targets, sources, occupation, offsets):
    scaled = sources * jnp.sqrt(occupation.astype(jnp.float32) * 0.5)[:, None]
    by_block = scaled.reshape(GROUPS, CYCLE, SRC_DEV, CELLS)
    target_blocks = targets.reshape(CYCLE, TGT_DEV, CELLS)
    kernel_grid = screened_kernel(NG)

    def one_block(inputs):
        block_index, target_rows = inputs
        accumulated = jnp.zeros((TGT_DEV, CELLS), jnp.float32)
        for group_index in range(GROUPS):
            for stop_index in range(STOPS):
                source_block = ((block_index - offsets[group_index] - stop_index) % CYCLE).astype(jnp.int32)
                partners = lax.dynamic_index_in_dim(by_block[group_index], source_block, 0, keepdims=False)
                density = target_rows[:, None, :] * partners[None, :, :]
                potential = pair_potential(density, kernel_grid)
                accumulated = accumulated + lax.optimization_barrier(jnp.sum(potential * partners[None, :, :], axis=1))
        return -accumulated
    result = lax.map(one_block, (jnp.arange(CYCLE, dtype=jnp.int32), target_blocks))
    return result.reshape(CYCLE * TGT_DEV, CELLS)
```

```python
import functools
import math

import jax
import jax.numpy as jnp
import numpy as np
from jax import lax
from jax.experimental import pallas as pl
from jax.experimental.pallas import tpu as pltpu
from jax.sharding import PartitionSpec as P

NG = 64
STOPS = 4
LANES = 128

box_length = 16.0
screen_square = 0.25


def split_np(table):
    high = table.astype(jnp.bfloat16)
    low = (table - high.astype(np.float64)).astype(jnp.bfloat16)
    return high, low


def stacked(table):
    high, low = split_np(table)
    return np.concatenate(
        [np.concatenate([high, high], axis=1), np.concatenate([low, low], axis=1)], axis=0
    )


def tables():
    counter = np.arange(NG)
    angle = 2.0 * np.pi * (counter[:, None] * counter[None, :] % NG) / NG
    cas = (np.cos(angle) + np.sin(angle)) / math.sqrt(NG)
    order = np.concatenate([counter[0::2], counter[1::2]])
    along_x = stacked(cas)
    along_y = stacked(cas[:, order])
    back_y = stacked(cas[order, :])
    blocks = np.kron(np.eye(4), cas)
    z_high, z_low = split_np(blocks)
    freq = np.where(counter < NG // 2, counter, counter - NG)
    wave = (2.0 * np.pi * freq / box_length) ** 2
    plane = wave[:, None] + np.tile(wave, 2)[None, :] + screen_square
    return along_x, along_y, back_y, z_high, z_low, plane.astype(np.float32), wave.astype(np.float32)


def split(value):
    high = value.astype(jnp.bfloat16)
    low = (value - high.astype(jnp.float32)).astype(jnp.bfloat16)
    return high, low


def left(table, value):
    high, low = split(value)
    both = jnp.dot(
        table, jnp.concatenate([high, low], axis=0), preferred_element_type=jnp.float32
    )
    return both[:NG] + both[NG:]


def right(z_high, z_low, value):
    high, low = split(value)
    dot = functools.partial(jnp.dot, preferred_element_type=jnp.float32)
    return dot(high, z_high) + (dot(low, z_high) + dot(high, z_low))


HALF = NG // 2
XB = 4


def pair_kernel(count, has_prior, slots, wave, *refs):
    pool = refs[:count]
    refs = refs[count:]
    targets, along_x, along_y, back_y, z_high, z_low, plane = refs[:7]
    refs = refs[7:]
    if has_prior:
        prior, refs = refs[0], refs[1:]
    out, src, field, sems = refs

    for s in range(2):
        for i in range(count):
            @pl.when(slots[s] == i)
            def _():
                pltpu.make_async_copy(pool[i], src.at[s], sems.at[s]).start()
    for s in range(2):
        pltpu.make_async_copy(pool[0], src.at[s], sems.at[s]).wait()

    first = lax.broadcasted_iota(jnp.int32, (HALF, LANES), 1) < NG

    def interleave(a, b):
        even = jnp.where(first, a, pltpu.roll(b, NG, 1))
        odd = jnp.where(first, pltpu.roll(a, NG, 1), b)
        return even, odd

    def source_rows(s, x):
        v = src[s, pl.ds(pl.multiple_of(x * HALF, HALF), HALF), :]
        even, odd = interleave(v, v)
        return jnp.concatenate([even, odd], axis=0)

    def source_plane(x):
        return jnp.concatenate([source_rows(0, x), source_rows(1, x)], axis=1)

    def forward(step, carry):
        slabs = []
        for k in range(XB):
            x = step * XB + k
            rows = pl.ds(pl.multiple_of(x * HALF, HALF), HALF)
            even, odd = interleave(targets[0, rows, :], targets[1, rows, :])
            t = jnp.concatenate([even, odd], axis=0)
            slabs.append(jnp.concatenate([t, t], axis=1) * source_plane(x))
        lines = right(z_high[...], z_low[...], jnp.concatenate(slabs, axis=0))
        for k in range(XB):
            x = step * XB + k
            r = left(along_y[...], lines[k * NG : (k + 1) * NG])
            rows = pl.ds(pl.multiple_of(x * NG, NG), NG)
            field[0, rows, :] = r[:, :LANES]
            field[1, rows, :] = r[:, LANES:]
        return carry

    def middle(y, carry):
        rows = pl.ds(y, NG, stride=NG)
        v = jnp.concatenate([field[0, rows, :], field[1, rows, :]], axis=1)
        v = left(along_x[...], v)
        factor = (4.0 * math.pi) / (plane[...] + wave[y])
        v = left(along_x[...], v * jnp.concatenate([factor, factor], axis=1))
        field[0, rows, :] = v[:, :LANES]
        field[1, rows, :] = v[:, LANES:]
        return carry

    def backward(step, carry):
        slabs = []
        for k in range(XB):
            x = step * XB + k
            rows = pl.ds(pl.multiple_of(x * NG, NG), NG)
            v = jnp.concatenate([field[0, rows, :], field[1, rows, :]], axis=1)
            slabs.append(left(back_y[...], v))
        lines = right(z_high[...], z_low[...], jnp.concatenate(slabs, axis=0))
        for k in range(XB):
            x = step * XB + k
            v = lines[k * NG : (k + 1) * NG] * source_plane(x)
            v = v[:, :LANES] + v[:, LANES:]
            a, b = interleave(v[:HALF], v[HALF:])
            rows = pl.ds(pl.multiple_of(x * HALF, HALF), HALF)
            if has_prior:
                out[0, rows, :] = prior[0, rows, :] - a
                out[1, rows, :] = prior[1, rows, :] - b
            else:
                out[0, rows, :] = -a
                out[1, rows, :] = -b
        return carry

    lax.fori_loop(0, NG // XB, forward, 0)
    lax.fori_loop(0, NG, middle, 0, unroll=2)
    lax.fori_loop(0, NG // XB, backward, 0)


def exchange_terms(slots, pool, targets, prior, consts):
    *mats, wave = consts
    rows = targets.shape[1]
    smem = pl.BlockSpec(memory_space=pltpu.SMEM)
    vmem = pl.BlockSpec(memory_space=pltpu.VMEM)
    anywhere = pl.BlockSpec(memory_space=pl.ANY)
    extra = [] if prior is None else [prior]
    return pl.pallas_call(
        functools.partial(pair_kernel, len(pool), prior is not None),
        out_shape=jax.ShapeDtypeStruct(targets.shape, jnp.float32),
        in_specs=[smem, smem] + [anywhere] * len(pool) + [vmem] * (1 + len(mats) + len(extra)),
        out_specs=vmem,
        scratch_shapes=[
            pltpu.VMEM((2, rows, LANES), jnp.float32),
            pltpu.VMEM((2, NG * NG, LANES), jnp.float32),
            pltpu.SemaphoreType.DMA((2,)),
        ],
        compiler_params=pltpu.CompilerParams(vmem_limit_bytes=40 * 1024 * 1024),
        cost_estimate=pl.CostEstimate(
            flops=20_000_000_000, bytes_accessed=8_000_000, transcendentals=0
        ),
    )(slots, wave, *pool, targets, *mats, *extra)


def ring_order(count):
    return list(range(0, count, 2)) + list(range(1, count, 2))[::-1]


def arrival(count):
    order = ring_order(count)
    place = [order.index(i) for i in range(count)]
    worst = [0] * STOPS
    for b in range(count):
        for off in range(count):
            steps = []
            for k in range(STOPS):
                d = (place[b] - place[(b - off - k) % count]) % count
                steps.append(min(d, count - d))
            worst = [max(w, s) for w, s in zip(worst, sorted(steps))]
    return worst[1], worst[3]


def partner(value, axis, bit):
    return lax.ppermute(value, axis, [(i, i ^ bit) for i in range(lax.axis_size(axis))])


def gather_rows(quarter, axis):
    me = lax.axis_index(axis)
    count = lax.axis_size(axis)
    parts = {0: quarter}
    bit = count // 2
    while bit:
        for key, value in list(parts.items()):
            parts[key ^ bit] = partner(value, axis, bit)
        bit //= 2
    ordered = []
    keys = sorted(parts)
    level = [parts[k] for k in keys]
    bit = 1
    while bit < count:
        swap = (me // bit) % 2 == 1
        merged = []
        for i in range(0, len(level), 2):
            a, b = level[i], level[i + 1]
            merged.append(
                jnp.concatenate([jnp.where(swap, b, a), jnp.where(swap, a, b)], axis=1)
            )
        level = merged
        bit *= 2
    return level[0]


def scatter_rows(total, axis):
    me = lax.axis_index(axis)
    count = lax.axis_size(axis)
    targets, rows, lanes = total.shape
    value = total.reshape((targets, count, rows // count, lanes))
    bit = 1
    while bit < count:
        mine = (me // bit) % 2 == 1
        pairs = value.reshape((targets, value.shape[1] // 2, 2) + value.shape[2:])
        low, high = pairs[:, :, 0], pairs[:, :, 1]
        value = jnp.where(mine, high, low) + partner(jnp.where(mine, low, high), axis, bit)
        bit *= 2
    return value[:, 0]


def local(targets, sources, occupation, offsets):
    count = lax.axis_size("blk")
    target_count, cells = targets.shape[0], sources.shape[1]
    consts = [jnp.asarray(v) for v in tables()]
    scaled = sources * jnp.sqrt(occupation.astype(jnp.float32) * 0.5)[:, None]
    scaled = scaled.reshape(cells // LANES, LANES)
    quarter = targets.reshape(target_count, targets.shape[1] // LANES, LANES)
    whole = gather_rows(quarter, "grp")

    order = ring_order(count)
    up = [(order[i], order[(i + 1) % count]) for i in range(count)]
    down = [(b, a) for a, b in up]
    first_step, last_step = arrival(count)
    pool = [scaled]
    ahead = behind = scaled
    for step in range(1, count // 2 + 1):
        if step < count // 2:
            ahead = lax.ppermute(ahead, "blk", up)
            behind = lax.ppermute(behind, "blk", down)
            pool += [ahead, behind]
        else:
            half = scaled.shape[0] // 2
            upper = lax.ppermute(ahead[:half], "blk", up)
            lower = lax.ppermute(behind[half:], "blk", down)
            pool += [jnp.concatenate([upper, lower], axis=0)]

    place = np.zeros(count, np.int32)
    place[order] = np.arange(count)
    place = jnp.asarray(place)
    me = lax.axis_index("blk")
    offset = lax.dynamic_index_in_dim(offsets, lax.axis_index("grp"), 0, keepdims=False)
    block = (me - offset - jnp.arange(STOPS, dtype=jnp.int32)) % count
    back = (place[me] - place[block]) % count
    slot = jnp.where(
        back == 0, 0, jnp.where(back <= count // 2, 2 * back - 1, 2 * (count - back))
    ).astype(jnp.int32)
    rank = jnp.sum((slot[None, :] < slot[:, None]).astype(jnp.int32), axis=1)
    ranked = jnp.sum(
        jnp.where(rank[None, :] == jnp.arange(STOPS)[:, None], slot[None, :], 0), axis=1
    ).astype(jnp.int32)

    early = pool[: 2 * first_step + 1]
    late = pool[: 2 * last_step + 1]
    partial = exchange_terms(ranked[:2], early, whole, None, consts)
    total = exchange_terms(ranked[2:], late, whole, partial, consts)
    return scatter_rows(total, "grp").reshape(targets.shape)


def solution(mesh):
    in_specs = (P("blk", "grp"), P(("grp", "blk"), None), P(("grp", "blk")), P())
    out_specs = P("blk", "grp")
    return jax.shard_map(local, mesh=mesh, in_specs=in_specs, out_specs=out_specs, check_vma=False)
```

```python
import functools
import math

import jax
import jax.numpy as jnp
import numpy as np
from jax import lax
from jax.experimental import pallas as pl
from jax.experimental.pallas import tpu as pltpu
from jax.sharding import PartitionSpec as P

NG = 64
STOPS = 4
LANES = 128

box_length = 16.0
screen_square = 0.25


def split_np(table):
    high = table.astype(jnp.bfloat16)
    low = (table - high.astype(np.float64)).astype(jnp.bfloat16)
    return high, low


def stacked(table):
    high, low = split_np(table)
    return np.concatenate(
        [np.concatenate([high, high], axis=1), np.concatenate([low, low], axis=1)], axis=0
    )


def tables():
    counter = np.arange(NG)
    angle = 2.0 * np.pi * (counter[:, None] * counter[None, :] % NG) / NG
    cas = (np.cos(angle) + np.sin(angle)) / math.sqrt(NG)
    order = np.concatenate([counter[0::2], counter[1::2]])
    along_x = stacked(cas)
    along_y = stacked(cas[:, order])
    back_y = stacked(cas[order, :])
    z_high, z_low = split_np(np.kron(np.eye(4), cas))
    freq = np.where(counter < NG // 2, counter, counter - NG)
    wave = (2.0 * np.pi * freq / box_length) ** 2
    plane = wave[:, None] + np.tile(wave, 2)[None, :] + screen_square
    return along_x, along_y, back_y, z_high, z_low, plane.astype(np.float32), wave.astype(np.float32)


def split(value):
    high = value.astype(jnp.bfloat16)
    low = (value - high.astype(jnp.float32)).astype(jnp.bfloat16)
    return high, low


def left(table, value):
    high, low = split(value)
    both = jnp.dot(
        table, jnp.concatenate([high, low], axis=0), preferred_element_type=jnp.float32
    )
    return both[:NG] + both[NG:]


def right(z_high, z_low, value):
    high, low = split(value)
    dot = functools.partial(jnp.dot, preferred_element_type=jnp.float32)
    return dot(high, z_high) + (dot(low, z_high) + dot(high, z_low))


HALF = NG // 2
XB = 8
YB = 8
CALLS = ((0, 1), (1, 3), (3, 4))


def pair_kernel(count, has_prior, slots, wave, *refs):
    pool = refs[:count]
    refs = refs[count:]
    targets, along_x, along_y, back_y, z_high, z_low, plane = refs[:7]
    refs = refs[7:]
    if has_prior:
        prior, refs = refs[0], refs[1:]
    out, src, field, sems = refs
    ns = src.shape[0]
    xb, yb = XB * 2 // ns, YB * 2 // ns
    width = ns * LANES

    def wide(parts):
        return jnp.concatenate(parts, axis=1) if ns > 1 else parts[0]

    def load(rows):
        return wide([field[s, rows, :] for s in range(ns)])

    def store(rows, v):
        for s in range(ns):
            field[s, rows, :] = v[:, s * LANES : (s + 1) * LANES]

    for s in range(ns):
        for i in range(count):
            @pl.when(slots[s] == i)
            def _():
                pltpu.make_async_copy(pool[i], src.at[s], sems.at[s]).start()
    for s in range(ns):
        pltpu.make_async_copy(pool[0], src.at[s], sems.at[s]).wait()

    first = lax.broadcasted_iota(jnp.int32, (HALF, LANES), 1) < NG

    def interleave(a, b):
        even = jnp.where(first, a, pltpu.roll(b, NG, 1))
        odd = jnp.where(first, pltpu.roll(a, NG, 1), b)
        return even, odd

    def source_rows(s, x):
        v = src[s, pl.ds(pl.multiple_of(x * HALF, HALF), HALF), :]
        even, odd = interleave(v, v)
        return jnp.concatenate([even, odd], axis=0)

    def source_plane(x):
        return wide([source_rows(s, x) for s in range(ns)])

    def forward(step, carry):
        slabs = []
        for k in range(xb):
            x = step * xb + k
            rows = pl.ds(pl.multiple_of(x * HALF, HALF), HALF)
            even, odd = interleave(targets[0, rows, :], targets[1, rows, :])
            t = jnp.concatenate([even, odd], axis=0)
            slabs.append(wide([t] * ns) * source_plane(x))
        lines = right(z_high[:width, :width], z_low[:width, :width], jnp.concatenate(slabs, axis=0))
        for k in range(xb):
            x = step * xb + k
            rows = pl.ds(pl.multiple_of(x * NG, NG), NG)
            store(rows, left(along_y[...], lines[k * NG : (k + 1) * NG]))
        return carry

    def middle(step, carry):
        group = [step * yb + k for k in range(yb)]
        slabs = []
        for y in group:
            rows = pl.ds(y, NG, stride=NG)
            slabs.append(load(rows))
        slabs = [left(along_x[...], v) for v in slabs]
        for k, y in enumerate(group):
            factor = (4.0 * math.pi) / (plane[...] + wave[y])
            slabs[k] = slabs[k] * wide([factor] * ns)
        slabs = [left(along_x[...], v) for v in slabs]
        for y, v in zip(group, slabs):
            rows = pl.ds(y, NG, stride=NG)
            store(rows, v)
        return carry

    def backward(step, carry):
        slabs = []
        for k in range(xb):
            x = step * xb + k
            rows = pl.ds(pl.multiple_of(x * NG, NG), NG)
            slabs.append(left(back_y[...], load(rows)))
        lines = right(z_high[:width, :width], z_low[:width, :width], jnp.concatenate(slabs, axis=0))
        for k in range(xb):
            x = step * xb + k
            v = lines[k * NG : (k + 1) * NG] * source_plane(x)
            v = sum(v[:, s * LANES : (s + 1) * LANES] for s in range(ns))
            a, b = interleave(v[:HALF], v[HALF:])
            rows = pl.ds(pl.multiple_of(x * HALF, HALF), HALF)
            if has_prior:
                out[0, rows, :] = prior[0, rows, :] - a
                out[1, rows, :] = prior[1, rows, :] - b
            else:
                out[0, rows, :] = -a
                out[1, rows, :] = -b
        return carry

    lax.fori_loop(0, NG // xb, forward, 0)
    lax.fori_loop(0, NG // yb, middle, 0)
    lax.fori_loop(0, NG // xb, backward, 0)


def exchange_terms(slots, pool, targets, prior, consts):
    *mats, wave = consts
    rows = targets.shape[1]
    ns = slots.shape[0]
    smem = pl.BlockSpec(memory_space=pltpu.SMEM)
    vmem = pl.BlockSpec(memory_space=pltpu.VMEM)
    anywhere = pl.BlockSpec(memory_space=pl.ANY)
    extra = [] if prior is None else [prior]
    return pl.pallas_call(
        functools.partial(pair_kernel, len(pool), prior is not None),
        out_shape=jax.ShapeDtypeStruct(targets.shape, jnp.float32),
        in_specs=[smem, smem] + [anywhere] * len(pool) + [vmem] * (1 + len(mats) + len(extra)),
        out_specs=vmem,
        scratch_shapes=[
            pltpu.VMEM((ns, rows, LANES), jnp.float32),
            pltpu.VMEM((ns, NG * NG, LANES), jnp.float32),
            pltpu.SemaphoreType.DMA((ns,)),
        ],
        compiler_params=pltpu.CompilerParams(vmem_limit_bytes=40 * 1024 * 1024),
        cost_estimate=pl.CostEstimate(
            flops=10_000_000_000 * ns, bytes_accessed=8_000_000, transcendentals=0
        ),
    )(slots, wave, *pool, targets, *mats, *extra)


def ring_order(count):
    return list(range(0, count, 2)) + list(range(1, count, 2))[::-1]


def arrival(count):
    order = ring_order(count)
    place = [order.index(i) for i in range(count)]
    worst = [0] * STOPS
    for b in range(count):
        for off in range(count):
            steps = []
            for k in range(STOPS):
                d = (place[b] - place[(b - off - k) % count]) % count
                steps.append(min(d, count - d))
            worst = [max(w, s) for w, s in zip(worst, sorted(steps))]
    return worst


def partner(value, axis, bit):
    return lax.ppermute(value, axis, [(i, i ^ bit) for i in range(lax.axis_size(axis))])


def gather_rows(quarter, axis):
    me = lax.axis_index(axis)
    count = lax.axis_size(axis)
    parts = {0: quarter}
    bit = count // 2
    while bit:
        for key, value in list(parts.items()):
            parts[key ^ bit] = partner(value, axis, bit)
        bit //= 2
    ordered = []
    keys = sorted(parts)
    level = [parts[k] for k in keys]
    bit = 1
    while bit < count:
        swap = (me // bit) % 2 == 1
        merged = []
        for i in range(0, len(level), 2):
            a, b = level[i], level[i + 1]
            merged.append(
                jnp.concatenate([jnp.where(swap, b, a), jnp.where(swap, a, b)], axis=1)
            )
        level = merged
        bit *= 2
    return level[0]


def scatter_rows(total, axis):
    me = lax.axis_index(axis)
    count = lax.axis_size(axis)
    targets, rows, lanes = total.shape
    value = total.reshape((targets, count, rows // count, lanes))
    bit = 1
    while bit < count:
        mine = (me // bit) % 2 == 1
        pairs = value.reshape((targets, value.shape[1] // 2, 2) + value.shape[2:])
        low, high = pairs[:, :, 0], pairs[:, :, 1]
        value = jnp.where(mine, high, low) + partner(jnp.where(mine, low, high), axis, bit)
        bit *= 2
    return value[:, 0]


def local(targets, sources, occupation, offsets):
    count = lax.axis_size("blk")
    target_count, cells = targets.shape[0], sources.shape[1]
    consts = [jnp.asarray(v) for v in tables()]
    scaled = sources * jnp.sqrt(occupation.astype(jnp.float32) * 0.5)[:, None]
    scaled = scaled.reshape(cells // LANES, LANES)
    quarter = targets.reshape(target_count, targets.shape[1] // LANES, LANES)
    whole = gather_rows(quarter, "grp")

    order = ring_order(count)
    up = [(order[i], order[(i + 1) % count]) for i in range(count)]
    down = [(b, a) for a, b in up]
    worst = arrival(count)
    pool = [scaled]
    ahead = behind = scaled
    for step in range(1, count // 2 + 1):
        if step < count // 2:
            ahead = lax.ppermute(ahead, "blk", up)
            behind = lax.ppermute(behind, "blk", down)
            pool += [ahead, behind]
        else:
            half = scaled.shape[0] // 2
            upper = lax.ppermute(ahead[:half], "blk", up)
            lower = lax.ppermute(behind[half:], "blk", down)
            pool += [jnp.concatenate([upper, lower], axis=0)]

    place = np.zeros(count, np.int32)
    place[order] = np.arange(count)
    place = jnp.asarray(place)
    me = lax.axis_index("blk")
    offset = lax.dynamic_index_in_dim(offsets, lax.axis_index("grp"), 0, keepdims=False)
    block = (me - offset - jnp.arange(STOPS, dtype=jnp.int32)) % count
    back = (place[me] - place[block]) % count
    slot = jnp.where(
        back == 0, 0, jnp.where(back <= count // 2, 2 * back - 1, 2 * (count - back))
    ).astype(jnp.int32)
    rank = jnp.sum((slot[None, :] < slot[:, None]).astype(jnp.int32), axis=1)
    ranked = jnp.sum(
        jnp.where(rank[None, :] == jnp.arange(STOPS)[:, None], slot[None, :], 0), axis=1
    ).astype(jnp.int32)

    total = None
    for first, end in CALLS:
        there = pool[: 2 * worst[end - 1] + 1]
        total = exchange_terms(ranked[first:end], there, whole, total, consts)
    return scatter_rows(total, "grp").reshape(targets.shape)


def solution(mesh):
    in_specs = (P("blk", "grp"), P(("grp", "blk"), None), P(("grp", "blk")), P())
    out_specs = P("blk", "grp")
    return jax.shard_map(local, mesh=mesh, in_specs=in_specs, out_specs=out_specs, check_vma=False)
```

```python
import functools
import math

import jax
import jax.numpy as jnp
import numpy as np
from jax import lax
from jax.experimental import pallas as pl
from jax.experimental.pallas import tpu as pltpu
from jax.sharding import PartitionSpec as P

NG = 64
STOPS = 4
LANES = 128

box_length = 16.0
screen_square = 0.25


def split_np(table):
    high = table.astype(jnp.bfloat16)
    low = (table - high.astype(np.float64)).astype(jnp.bfloat16)
    return high, low


def stacked(table):
    high, low = split_np(table)
    return np.concatenate(
        [np.concatenate([high, high], axis=1), np.concatenate([low, low], axis=1)], axis=0
    )


def tables():
    counter = np.arange(NG)
    angle = 2.0 * np.pi * (counter[:, None] * counter[None, :] % NG) / NG
    cas = (np.cos(angle) + np.sin(angle)) / math.sqrt(NG)
    order = np.concatenate([counter[0::2], counter[1::2]])
    along_x = stacked(cas)
    along_y = stacked(cas[:, order])
    back_y = stacked(cas[order, :])
    z_high, z_low = split_np(np.kron(np.eye(4), cas))
    freq = np.where(counter < NG // 2, counter, counter - NG)
    wave = (2.0 * np.pi * freq / box_length) ** 2
    plane = wave[:, None] + np.tile(wave, 2)[None, :] + screen_square
    return along_x, along_y, back_y, z_high, z_low, plane.astype(np.float32), wave.astype(np.float32)


def split(value):
    high = value.astype(jnp.bfloat16)
    low = (value - high.astype(jnp.float32)).astype(jnp.bfloat16)
    return high, low


def left(table, value):
    high, low = split(value)
    both = jnp.dot(
        table, jnp.concatenate([high, low], axis=0), preferred_element_type=jnp.float32
    )
    return both[:NG] + both[NG:]


def right(z_high, z_low, value):
    high, low = split(value)
    dot = functools.partial(jnp.dot, preferred_element_type=jnp.float32)
    return dot(high, z_high) + (dot(low, z_high) + dot(high, z_low))


HALF = NG // 2
XB = 16
YB = 8
CALLS = ((0, 1), (1, 3), (3, 4))


def pair_kernel(count, has_prior, slots, wave, *refs):
    pool = refs[:count]
    refs = refs[count:]
    targets, along_x, along_y, back_y, z_high, z_low, plane = refs[:7]
    refs = refs[7:]
    if has_prior:
        prior, refs = refs[0], refs[1:]
    out, src, field, sems = refs
    ns = src.shape[0]
    xb, yb = XB * 2 // ns, YB * 2 // ns
    width = ns * LANES

    def wide(parts):
        return jnp.concatenate(parts, axis=1) if ns > 1 else parts[0]

    def load(rows):
        return wide([field[s, rows, :] for s in range(ns)])

    def store(rows, v):
        for s in range(ns):
            field[s, rows, :] = v[:, s * LANES : (s + 1) * LANES]

    for s in range(ns):
        for i in range(count):
            @pl.when(slots[s] == i)
            def _():
                pltpu.make_async_copy(pool[i], src.at[s], sems.at[s]).start()
    for s in range(ns):
        pltpu.make_async_copy(pool[0], src.at[s], sems.at[s]).wait()

    first = lax.broadcasted_iota(jnp.int32, (HALF, LANES), 1) < NG

    def interleave(a, b):
        even = jnp.where(first, a, pltpu.roll(b, NG, 1))
        odd = jnp.where(first, pltpu.roll(a, NG, 1), b)
        return even, odd

    def source_rows(s, x):
        v = src[s, pl.ds(pl.multiple_of(x * HALF, HALF), HALF), :]
        even, odd = interleave(v, v)
        return jnp.concatenate([even, odd], axis=0)

    def source_plane(x):
        return wide([source_rows(s, x) for s in range(ns)])

    def forward(step, carry):
        slabs = []
        for k in range(xb):
            x = step * xb + k
            rows = pl.ds(pl.multiple_of(x * HALF, HALF), HALF)
            even, odd = interleave(targets[0, rows, :], targets[1, rows, :])
            t = jnp.concatenate([even, odd], axis=0)
            slabs.append(wide([t] * ns) * source_plane(x))
        lines = right(z_high[:width, :width], z_low[:width, :width], jnp.concatenate(slabs, axis=0))
        for k in range(xb):
            x = step * xb + k
            rows = pl.ds(pl.multiple_of(x * NG, NG), NG)
            store(rows, left(along_y[...], lines[k * NG : (k + 1) * NG]))
        return carry

    def middle(step, carry):
        group = [step * yb + k for k in range(yb)]
        slabs = []
        for y in group:
            rows = pl.ds(y, NG, stride=NG)
            slabs.append(load(rows))
        slabs = [left(along_x[...], v) for v in slabs]
        for k, y in enumerate(group):
            factor = (4.0 * math.pi) / (plane[...] + wave[y])
            slabs[k] = slabs[k] * wide([factor] * ns)
        slabs = [left(along_x[...], v) for v in slabs]
        for y, v in zip(group, slabs):
            rows = pl.ds(y, NG, stride=NG)
            store(rows, v)
        return carry

    def backward(step, carry):
        slabs = []
        for k in range(xb):
            x = step * xb + k
            rows = pl.ds(pl.multiple_of(x * NG, NG), NG)
            slabs.append(left(back_y[...], load(rows)))
        lines = right(z_high[:width, :width], z_low[:width, :width], jnp.concatenate(slabs, axis=0))
        for k in range(xb):
            x = step * xb + k
            v = lines[k * NG : (k + 1) * NG] * source_plane(x)
            v = sum(v[:, s * LANES : (s + 1) * LANES] for s in range(ns))
            a, b = interleave(v[:HALF], v[HALF:])
            rows = pl.ds(pl.multiple_of(x * HALF, HALF), HALF)
            if has_prior:
                out[0, rows, :] = prior[0, rows, :] - a
                out[1, rows, :] = prior[1, rows, :] - b
            else:
                out[0, rows, :] = -a
                out[1, rows, :] = -b
        return carry

    lax.fori_loop(0, NG // xb, forward, 0)
    lax.fori_loop(0, NG // yb, middle, 0)
    lax.fori_loop(0, NG // xb, backward, 0)


def exchange_terms(slots, pool, targets, prior, consts):
    *mats, wave = consts
    rows = targets.shape[1]
    ns = slots.shape[0]
    smem = pl.BlockSpec(memory_space=pltpu.SMEM)
    vmem = pl.BlockSpec(memory_space=pltpu.VMEM)
    anywhere = pl.BlockSpec(memory_space=pl.ANY)
    extra = [] if prior is None else [prior]
    return pl.pallas_call(
        functools.partial(pair_kernel, len(pool), prior is not None),
        out_shape=jax.ShapeDtypeStruct(targets.shape, jnp.float32),
        in_specs=[smem, smem] + [anywhere] * len(pool) + [vmem] * (1 + len(mats) + len(extra)),
        out_specs=vmem,
        scratch_shapes=[
            pltpu.VMEM((ns, rows, LANES), jnp.float32),
            pltpu.VMEM((ns, NG * NG, LANES), jnp.float32),
            pltpu.SemaphoreType.DMA((ns,)),
        ],
        compiler_params=pltpu.CompilerParams(vmem_limit_bytes=40 * 1024 * 1024),
        cost_estimate=pl.CostEstimate(
            flops=10_000_000_000 * ns, bytes_accessed=8_000_000, transcendentals=0
        ),
    )(slots, wave, *pool, targets, *mats, *extra)


def ring_order(count):
    return list(range(0, count, 2)) + list(range(1, count, 2))[::-1]


def arrival(count):
    order = ring_order(count)
    place = [order.index(i) for i in range(count)]
    worst = [0] * STOPS
    for b in range(count):
        for off in range(count):
            steps = []
            for k in range(STOPS):
                d = (place[b] - place[(b - off - k) % count]) % count
                steps.append(min(d, count - d))
            worst = [max(w, s) for w, s in zip(worst, sorted(steps))]
    return worst


def partner(value, axis, bit):
    return lax.ppermute(value, axis, [(i, i ^ bit) for i in range(lax.axis_size(axis))])


def gather_rows(quarter, axis):
    me = lax.axis_index(axis)
    count = lax.axis_size(axis)
    parts = {0: quarter}
    bit = count // 2
    while bit:
        for key, value in list(parts.items()):
            parts[key ^ bit] = partner(value, axis, bit)
        bit //= 2
    ordered = []
    keys = sorted(parts)
    level = [parts[k] for k in keys]
    bit = 1
    while bit < count:
        swap = (me // bit) % 2 == 1
        merged = []
        for i in range(0, len(level), 2):
            a, b = level[i], level[i + 1]
            merged.append(
                jnp.concatenate([jnp.where(swap, b, a), jnp.where(swap, a, b)], axis=1)
            )
        level = merged
        bit *= 2
    return level[0]


def scatter_rows(total, axis):
    me = lax.axis_index(axis)
    count = lax.axis_size(axis)
    targets, rows, lanes = total.shape
    value = total.reshape((targets, count, rows // count, lanes))
    bit = 1
    while bit < count:
        mine = (me // bit) % 2 == 1
        pairs = value.reshape((targets, value.shape[1] // 2, 2) + value.shape[2:])
        low, high = pairs[:, :, 0], pairs[:, :, 1]
        value = jnp.where(mine, high, low) + partner(jnp.where(mine, low, high), axis, bit)
        bit *= 2
    return value[:, 0]


def local(targets, sources, occupation, offsets):
    count = lax.axis_size("blk")
    target_count, cells = targets.shape[0], sources.shape[1]
    consts = [jnp.asarray(v) for v in tables()]
    scaled = sources * jnp.sqrt(occupation.astype(jnp.float32) * 0.5)[:, None]
    scaled = scaled.reshape(cells // LANES, LANES)
    quarter = targets.reshape(target_count, targets.shape[1] // LANES, LANES)
    whole = gather_rows(quarter, "grp")

    order = ring_order(count)
    up = [(order[i], order[(i + 1) % count]) for i in range(count)]
    down = [(b, a) for a, b in up]
    worst = arrival(count)
    pool = [scaled]
    ahead = behind = scaled
    for step in range(1, count // 2 + 1):
        if step < count // 2:
            ahead = lax.ppermute(ahead, "blk", up)
            behind = lax.ppermute(behind, "blk", down)
            pool += [ahead, behind]
        else:
            half = scaled.shape[0] // 2
            upper = lax.ppermute(ahead[:half], "blk", up)
            lower = lax.ppermute(behind[half:], "blk", down)
            pool += [jnp.concatenate([upper, lower], axis=0)]

    place = np.zeros(count, np.int32)
    place[order] = np.arange(count)
    place = jnp.asarray(place)
    me = lax.axis_index("blk")
    offset = lax.dynamic_index_in_dim(offsets, lax.axis_index("grp"), 0, keepdims=False)
    block = (me - offset - jnp.arange(STOPS, dtype=jnp.int32)) % count
    back = (place[me] - place[block]) % count
    slot = jnp.where(
        back == 0, 0, jnp.where(back <= count // 2, 2 * back - 1, 2 * (count - back))
    ).astype(jnp.int32)
    rank = jnp.sum((slot[None, :] < slot[:, None]).astype(jnp.int32), axis=1)
    ranked = jnp.sum(
        jnp.where(rank[None, :] == jnp.arange(STOPS)[:, None], slot[None, :], 0), axis=1
    ).astype(jnp.int32)

    total = None
    for first, end in CALLS:
        there = pool[: 2 * worst[end - 1] + 1]
        total = exchange_terms(ranked[first:end], there, whole, total, consts)
    return scatter_rows(total, "grp").reshape(targets.shape)


def solution(mesh):
    in_specs = (P("blk", "grp"), P(("grp", "blk"), None), P(("grp", "blk")), P())
    out_specs = P("blk", "grp")
    return jax.shard_map(local, mesh=mesh, in_specs=in_specs, out_specs=out_specs, check_vma=False)
```
